256 devices in a mesh: row: 16 (over x_lo, y, core), col: 16 (over z, x_hi).
Axes of the slice: x: 4 (x_hi: 2, x_lo: 2; x = x_hi * 2 + x_lo), y: 4, z: 8, core: 2. Of those that a mesh axis runs over, the one named last changes fastest.
Arguments:
- row_points: bfloat16 [16384, 64], P(('row', 'col')), may hold values from -6 to 6, as said below
- col_points: bfloat16 [131072, 64], P(('col', 'row')), may hold values from -6 to 6, as said below
- row_vectors: bfloat16 [16384, 64], P(('row', 'col')), may hold values from -1 to 1
- col_vectors: bfloat16 [131072, 64], P(('col', 'row')), may hold values from -0.375 to 0.375
- weight_in: bfloat16 [64, 512], replicated, may hold values from -0.75 to 0.75
- bias_in: float32 [512], replicated, may hold values from -3 to 3
- weight_mid: bfloat16 [512, 512], replicated, may hold values from -0.75 to 0.75
- bias_mid: float32 [512], replicated, may hold values from -3 to 3
- weight_out: bfloat16 [512, 256], replicated, may hold values from -0.75 to 0.75
- ard_scales: float32 [256], replicated, may hold values from 0.002 to 0.01
- signal_scale: float32 [1], replicated, may hold values from 0.5 to 2
Outputs:
- row_result: float32 [16384, 64], P(('row', 'col'))
- col_result: float32 [131072, 64], P(('col', 'row'))
The draws below stay inside these ranges and needn't reach their ends.
Inputs may be any that keep to these rules, and one draw needn't show every extreme that they name: `row_points`: each row point's input lies near one of 512 centres that row and column points share; which centre is not given. `col_points`: each column point's input lies near one of the same 512 centres; which centre is not given.
All inputs are finite; a program needn't handle non-finite values.
Results may differ from the reference program's by a relative error of at most 0.0041.
Values may be sent and summed in bfloat16 or wider, within the bound.
A program may use at most 64 MiB of HBM per device.

```python
import math
import jax
import jax.numpy as jnp
from jax import lax

IN = 64
H = 512
D_EMB = 256
NVEC = 64
NROW = 16384
NCOL = 131072
CENTRES = 512


def shared_centres(key):
    centre_key = jax.random.fold_in(key, 7)
    return jax.random.truncated_normal(centre_key, -3.5, 3.5, (CENTRES, IN), jnp.float32)


def scattered_points(key, point_count, salt_value):
    centres = shared_centres(key)
    labels = jax.random.randint(jax.random.fold_in(key, salt_value), (point_count,), 0, CENTRES)
    near_centre = jnp.take(centres, labels, axis=0)
    jitter_key = jax.random.fold_in(key, salt_value + 1)
    jitter = 0.4 * jax.random.truncated_normal(jitter_key, -3.5, 3.5, (point_count, IN), jnp.float32)
    return (near_centre + jitter).astype(jnp.bfloat16)


def draw_row_points(key, part):
    return scattered_points(key, NROW, 11)


def draw_col_points(key, part):
    return scattered_points(key, NCOL, 23)


def steps_of(own_key, shape, pieces, smallest, top_value):
    level = 1.0
    for position, blocks in pieces:
        steps = jax.random.uniform(jax.random.fold_in(jax.random.fold_in(own_key, 6), position), (blocks,), jnp.float32, smallest / len(pieces), top_value / len(pieces))
        level = level * jnp.repeat(jnp.exp(steps), shape[position] // blocks).reshape((-1,) + (1,) * (len(shape) - 1 - position))
    return level


def scatter_about(own_key, extent, deviation, most, shards=(), kind=jnp.bfloat16):
    loudness = steps_of(own_key, extent, shards, -0.22, 0.18) if shards else 1.0
    entries = jax.random.normal(own_key, extent, jnp.float32) * deviation * loudness
    return jnp.minimum(jnp.maximum(entries, -most), most).astype(kind)


def setup_inputs(seed: int = 0) -> dict:
    arg_keys = jax.random.split(jax.random.key(seed), 12)
    return {
        "row_points": draw_row_points(jax.random.fold_in(arg_keys[11], 71), 0),
        "col_points": draw_col_points(jax.random.fold_in(arg_keys[11], 71), 0),
        "row_vectors": scatter_about(arg_keys[2], (NROW, NVEC), (max(NROW // CENTRES, 1)) ** -0.5, 1.0, ((0, 256),)),
        "col_vectors": scatter_about(arg_keys[3], (NCOL, NVEC), (max(NCOL // CENTRES, 1)) ** -0.5, 0.375, ((0, 256),)),
        "weight_in": scatter_about(arg_keys[4], (IN, H), IN ** -0.5, 0.75),
        "bias_in": scatter_about(arg_keys[5], (H,), 0.5, 3.0, (), jnp.float32),
        "weight_mid": scatter_about(arg_keys[6], (H, H), (H // 8) ** -0.5, 0.75),
        "bias_mid": scatter_about(arg_keys[7], (H,), 0.5, 3.0, (), jnp.float32),
        "weight_out": scatter_about(arg_keys[8], (H, D_EMB), (H // 8) ** -0.5, 0.75),
        "ard_scales": jnp.clip(jnp.exp(jax.random.uniform(arg_keys[9], (D_EMB,), jnp.float32, math.log(0.002), math.log(0.01))), 0.002, 0.01),
        "signal_scale": jnp.clip(jnp.exp(jax.random.uniform(arg_keys[10], (1,), jnp.float32, math.log(0.5), math.log(2.0))), 0.5, 2.0),
    }


def embed_points(points, weight_in, bias_in, weight_mid, bias_mid, weight_out, ard_scales):
    hidden_one = jnp.tanh(jnp.dot(points, weight_in, preferred_element_type=jnp.float32) + bias_in).astype(jnp.bfloat16)
    hidden_two = jnp.tanh(jnp.dot(hidden_one, weight_mid, preferred_element_type=jnp.float32) + bias_mid).astype(jnp.bfloat16)
    return (jnp.dot(hidden_two, weight_out, preferred_element_type=jnp.float32) * jnp.sqrt(ard_scales)).astype(jnp.bfloat16)

def reference(row_points, col_points, row_vectors, col_vectors, weight_in, bias_in, weight_mid, bias_mid, weight_out, ard_scales, signal_scale):
    row_feats = embed_points(row_points, weight_in, bias_in, weight_mid, bias_mid, weight_out, ard_scales)
    col_feats = embed_points(col_points, weight_in, bias_in, weight_mid, bias_mid, weight_out, ard_scales)
    row_sq = lax.optimization_barrier(jnp.sum(jnp.square(row_feats.astype(jnp.float32)), axis=1))
    col_sq = lax.optimization_barrier(jnp.sum(jnp.square(col_feats.astype(jnp.float32)), axis=1))
    width_cols = math.gcd(NCOL, 1024)
    groups = NCOL // width_cols
    feat_groups = col_feats.reshape(groups, width_cols, D_EMB)
    vector_groups = col_vectors.reshape(groups, width_cols, NVEC)
    square_groups = col_sq.reshape(groups, width_cols)

    def visit(totals, inputs):
        feats_now, vectors_now, squares_now = inputs
        inner_prod = lax.dot_general(row_feats, feats_now, (((1,), (1,)), ((), ())), preferred_element_type=jnp.float32)
        kernel = jnp.exp(inner_prod - 0.5 * row_sq[:, None] - 0.5 * squares_now[None, :]).astype(jnp.bfloat16)
        totals = totals + jnp.dot(kernel, vectors_now, preferred_element_type=jnp.float32)
        col_part = lax.dot_general(kernel, row_vectors, (((0,), (0,)), ((), ())), preferred_element_type=jnp.float32)
        return (totals, col_part)
    row_total, col_parts = lax.scan(visit, jnp.zeros((NROW, NVEC), jnp.float32), (feat_groups, vector_groups, square_groups))
    return (signal_scale[0] * row_total, signal_scale[0] * col_parts.reshape(NCOL, NVEC))
```

```python
import jax
import jax.numpy as jnp
from jax import lax
from jax.experimental import pallas as pl
from jax.experimental.pallas import tpu as pltpu
from jax.sharding import PartitionSpec as P

MESH = pl.DeviceIdType.MESH
F32 = jnp.float32
BF16 = jnp.bfloat16
LOG2E = 1.4426950408889634

NX, NY, NZ = (4, 4, 8)
Z_OFF = (0, 4, -1, 1, -2, 2, -3, 3)
Y_OFF = (0, -1, 1, 2)
X_OFF = (0, -1, 1, 2)
MINUS = {0: 0, 1: 2, 2: 4, 3: 6, 4: 1}
PLUS = {0: 0, 1: 3, 2: 5, 3: 7}


def kernel(
    rp, rv, cp, cv, w1, b1, w2, b2, w3, ard, sig,
    rout, cout,
    w1p, xr, xc, rf, fc, vrt, vct, rn, cn, pt, oc, rsend, rrecv, csend, crecv,
    y_s, y_r, z_s, z_r, x_s, x_r, p_s, p_r, rr_s, rr_r, cc_s, cc_r,
):
    row, col = (lax.axis_index("row"), lax.axis_index("col"))
    core = lax.rem(row, 2)
    y = lax.rem(lax.div(row, 2), NY)
    x = lax.div(row, 2 * NY) + 2 * lax.rem(col, 2)
    z = lax.div(col, 2)

    def dev(dx=0, dy=0, dz=0, other=0):
        px = lax.rem(x + (dx + NX), NX)
        py = lax.rem(y + (dy + NY), NY)
        pz = lax.rem(z + (dz + NZ), NZ)
        pc = 1 - core if other else core
        return (lax.rem(px, 2) * (2 * NY) + py * 2 + pc, pz * 2 + lax.div(px, 2))

    def send(src, dst, s, r, to):
        c = pltpu.make_async_remote_copy(
            src_ref=src, dst_ref=dst, send_sem=s, recv_sem=r, device_id=to, device_id_type=MESH
        )
        c.start()
        return c

    peers = [dict(dy=dy, dz=dz) for dz in Z_OFF for dy in Y_OFF if (dy, dz) != (0, 0)]
    peers += [dict(dx=dx, other=o) for o in (0, 1) for dx in X_OFF if (dx, o) != (0, 0)]
    barrier = pltpu.get_barrier_semaphore()
    for q in peers:
        pl.semaphore_signal(barrier, inc=1, device_id=dev(**q), device_id_type=MESH)

    xr[0:64, :] = jnp.concatenate([rp[...], rv[...]], axis=1)
    xc[0:512, :] = jnp.concatenate([cp[...], cv[...]], axis=1)
    w1p[0:64, :] = w1[...]
    w1p[64:128, :] = jnp.zeros_like(w1)
    pl.semaphore_wait(barrier, len(peers))

    waits = []
    ys = []
    for j, dy in enumerate(Y_OFF):
        if j:
            ys.append(
                send(xr.at[0:64], xr.at[64 * j : 64 * j + 64], y_s.at[j], y_r.at[j], dev(dy=-dy))
            )
    xs = []
    for j, dx in enumerate(X_OFF):
        if j:
            xs.append(
                send(xc.at[0:512], xc.at[512 * j : 512 * j + 512], x_s.at[j], x_r.at[j], dev(dx=-dx))
            )
    for c in ys:
        c.wait()
    for step in range(1, 5):
        now = []
        for table, d in ((MINUS, 1), (PLUS, -1)):
            if step in table:
                a, b = (table[step - 1] * 256, table[step] * 256)
                i = table[step]
                now.append(
                    send(xr.at[a : a + 256], xr.at[b : b + 256], z_s.at[i], z_r.at[i], dev(dz=d))
                )
        for c in now:
            c.wait()
    for c in xs:
        c.wait()

    def embed(raw):
        h = jnp.tanh(jnp.dot(raw, w1p[...], preferred_element_type=F32) + b1[...]).astype(BF16)
        h = jnp.tanh(jnp.dot(h, w2[...], preferred_element_type=F32) + b2[...]).astype(BF16)
        out = jnp.dot(h, w3[...], preferred_element_type=F32) * jnp.sqrt(ard[...])
        return out.astype(BF16)

    def half_sq(feats):
        f = feats.astype(F32)
        return (-0.5 * LOG2E) * jnp.sum(f * f, axis=1, keepdims=True)

    def embed_cols(i, _):
        at = pl.multiple_of(i * 512, 512)
        raw = xc[pl.ds(at, 512), :]
        fc[pl.ds(at, 512), :] = embed(raw)
        vct[:, pl.ds(at, 512)] = raw.T[64:128, :]
        return 0

    lax.fori_loop(0, 4, embed_cols, 0)
    part = [
        send(fc.at[0:2048], fc.at[2048:4096], p_s.at[0], p_r.at[0], dev(other=1)),
        send(vct.at[:, 0:2048], vct.at[:, 2048:4096], p_s.at[1], p_r.at[1], dev(other=1)),
    ]

    def embed_rows(i, _):
        at = pl.multiple_of(i * 512, 512)
        raw = xr[pl.ds(at, 512), :]
        feats = embed(raw)
        rf[pl.ds(at, 512), :] = feats
        vrt[:, pl.ds(at, 512)] = raw.T[64:128, :]
        rn[:, pl.ds(at, 512)] = jnp.broadcast_to(half_sq(feats), (512, 128)).T[0:8, :]
        return 0

    lax.fori_loop(0, 4, embed_rows, 0)
    for c in part:
        c.wait()

    def col_norms(i, _):
        at = pl.multiple_of(i * 512, 512)
        cn[pl.ds(at, 512), :] = jnp.broadcast_to(half_sq(fc[pl.ds(at, 512), :]), (512, 128))
        return 0

    lax.fori_loop(0, 8, col_norms, 0)
    oc[...] = jnp.zeros_like(oc)

    def panel(i, _):
        at = pl.multiple_of(i * 512, 512)
        inner = lax.dot_general(
            fc[...], rf[pl.ds(at, 512), :], (((1,), (1,)), ((), ())), preferred_element_type=F32
        )
        norms = jnp.concatenate([cn[...]] * 4, axis=1)
        k = jnp.exp2(inner * LOG2E + norms + rn[0:1, pl.ds(at, 512)]).astype(BF16)
        rows = jnp.dot(vct[...], k, preferred_element_type=F32)
        pt[...] = k.T
        oc[...] += jnp.dot(vrt[:, pl.ds(at, 512)], pt[...], preferred_element_type=F32)
        rt = rows.T.astype(BF16)
        for j in range(8):
            rsend[i * 8 + j] = jnp.concatenate(
                [rt[64 * j : 64 * j + 32], rt[64 * j + 32 : 64 * j + 64]], axis=1
            )
        return 0

    lax.fori_loop(0, 4, panel, 0)
    csend[...] = oc[...].astype(BF16)

    out = []
    for i, dz in enumerate(Z_OFF):
        for j, dy in enumerate(Y_OFF):
            n = 4 * i + j
            if n:
                out.append(
                    send(rsend.at[n], rrecv.at[n], rr_s.at[n], rr_r.at[n], dev(dy=dy, dz=dz))
                )
    for o in (0, 1):
        for j, dx in enumerate(X_OFF):
            n = 4 * o + j
            if n:
                out.append(
                    send(
                        csend.at[:, 512 * n : 512 * n + 512], crecv.at[n],
                        cc_s.at[n], cc_r.at[n], dev(dx=dx, other=o),
                    )
                )
    for c in out:
        c.wait()
    scale = sig[0]
    total = rsend[0].astype(F32)
    for n in range(1, 32):
        total += rrecv[n].astype(F32)
    total = total * scale
    rout[0:32, :] = total[:, 0:64]
    rout[32:64, :] = total[:, 64:128]
    total = csend[:, 0:512].astype(F32)
    for n in range(1, 8):
        total += crecv[n].astype(F32)
    cout[...] = (total * scale).T


def body(rp, cp, rv, cv, w1, b1, w2, b2, w3, ard, sig):
    vmem = pl.BlockSpec(memory_space=pltpu.VMEM)
    dma = pltpu.SemaphoreType.DMA
    return pl.pallas_call(
        kernel,
        out_shape=(jax.ShapeDtypeStruct((64, 64), F32), jax.ShapeDtypeStruct((512, 64), F32)),
        in_specs=[vmem] * 10 + [pl.BlockSpec(memory_space=pltpu.SMEM)],
        out_specs=(vmem, vmem),
        scratch_shapes=[
            pltpu.VMEM((128, 512), BF16),
            pltpu.VMEM((2048, 128), BF16),
            pltpu.VMEM((2048, 128), BF16),
            pltpu.VMEM((2048, 256), BF16),
            pltpu.VMEM((4096, 256), BF16),
            pltpu.VMEM((64, 2048), BF16),
            pltpu.VMEM((64, 4096), BF16),
            pltpu.VMEM((8, 2048), F32),
            pltpu.VMEM((4096, 128), F32),
            pltpu.VMEM((512, 4096), BF16),
            pltpu.VMEM((64, 4096), F32),
            pltpu.VMEM((32, 32, 128), BF16),
            pltpu.VMEM((32, 32, 128), BF16),
            pltpu.VMEM((64, 4096), BF16),
            pltpu.VMEM((8, 64, 512), BF16),
            dma((4,)), dma((4,)), dma((8,)), dma((8,)), dma((4,)), dma((4,)),
            dma((2,)), dma((2,)), dma((32,)), dma((32,)), dma((8,)), dma((8,)),
        ],
        compiler_params=pltpu.CompilerParams(
            collective_id=0, has_side_effects=True, vmem_limit_bytes=62 * 2**20
        ),
    )(rp, rv, cp, cv, w1, b1.reshape(1, -1), w2, b2.reshape(1, -1), w3, ard.reshape(1, -1), sig)


def solution(mesh):
    rows, cols = (P(("row", "col"), None), P(("col", "row"), None))
    in_specs = (rows, cols, rows, cols) + (P(),) * 7
    return jax.shard_map(
        body, mesh=mesh, in_specs=in_specs, out_specs=(rows, cols), check_vma=False
    )
```

```python
import jax
import jax.numpy as jnp
from jax import lax
from jax.experimental import pallas as pl
from jax.experimental.pallas import tpu as pltpu
from jax.sharding import PartitionSpec as P

MESH = pl.DeviceIdType.MESH
F32 = jnp.float32
BF16 = jnp.bfloat16
LOG2E = 1.4426950408889634

NX, NY, NZ = (4, 4, 8)
Z_OFF = (-3, 2, 4, 3, -2, 1, -1, 0)
Y_OFF = (0, -1, 1, 2)
X_OFF = (0, 1, -1, 2)
MINUS = {0: 7, 1: 6, 2: 4, 3: 0, 4: 2}
PLUS = {0: 7, 1: 5, 2: 1, 3: 3}


def kernel(
    rp, rv, cp, cv, w1, b1, w2, b2, w3, ard, sig,
    rout, cout,
    w1v, w2v, w3v, rpv, rvv, xr, xc, rf, fc, vrt, vct, rn, cn, pt, oc, orr,
    rsend, rrecv, csend, crecv,
    l_s, y_s, y_r, z_s, z_r, x_s, x_r, p_s, p_r, rr_s, rr_r, cc_s, cc_r,
):
    row, col = (lax.axis_index("row"), lax.axis_index("col"))
    core = lax.rem(row, 2)
    y = lax.rem(lax.div(row, 2), NY)
    x = lax.div(row, 2 * NY) + 2 * lax.rem(col, 2)
    z = lax.div(col, 2)

    def dev(dx=0, dy=0, dz=0, other=0):
        px = lax.rem(x + (dx + NX), NX)
        py = lax.rem(y + (dy + NY), NY)
        pz = lax.rem(z + (dz + NZ), NZ)
        pc = 1 - core if other else core
        return (lax.rem(px, 2) * (2 * NY) + py * 2 + pc, pz * 2 + lax.div(px, 2))

    sent = []

    def send(src, dst, s, r, to):
        c = pltpu.make_async_remote_copy(
            src_ref=src, dst_ref=dst, send_sem=s, recv_sem=r, device_id=to, device_id_type=MESH
        )
        c.start()
        sent.append(c)
        return c

    peers = [dict(other=1)] + [dict(dx=d) for d in (1, -1)]
    peers += [dict(dy=d) for d in (1, -1, 2)] + [dict(dz=d) for d in (1, -1)]
    barrier = pltpu.get_barrier_semaphore()
    for q in peers:
        pl.semaphore_signal(barrier, inc=1, device_id=dev(**q), device_id_type=MESH)

    local = []
    for i, (a, b) in enumerate(
        ((rp, rpv), (rv, rvv), (cp, xc.at[0, 0:64]), (cv, xc.at[0, 64:128]), (w1, w1v.at[0:64]),
         (w2, w2v), (w3, w3v))
    ):
        c = pltpu.make_async_copy(a, b, l_s.at[i])
        c.start()
        local.append(c)
    w1v[64:128, :] = jnp.zeros((64, 512), BF16)
    local[0].wait()
    local[1].wait()
    xr[1792:1856, :] = jnp.concatenate([rpv[...], rvv[...]], axis=1)
    local[2].wait()
    local[3].wait()
    pl.semaphore_wait(barrier, len(peers))

    ys = []
    for j, dy in enumerate(Y_OFF):
        if j:
            ys.append(
                send(
                    xr.at[1792:1856], xr.at[1792 + 64 * j : 1856 + 64 * j],
                    y_s.at[j], y_r.at[j], dev(dy=-dy),
                )
            )

    def half(slot, h):
        return xc.at[slot, :, 256 * h : 256 * h + 256]

    xs = {}
    for h in (0, 1):
        xs[2, h] = send(half(0, h), half(2, h), x_s.at[4 + h], x_r.at[4 + h], dev(dx=1))
        g = 1 - h
        xs[1, g] = send(half(0, g), half(1, g), x_s.at[2 + g], x_r.at[2 + g], dev(dx=-1))
    for c in local[4:]:
        c.wait()

    def embed(pre):
        h = jnp.tanh(pre + b1[...]).astype(BF16)
        h = jnp.tanh(jnp.dot(h, w2v[...], preferred_element_type=F32) + b2[...]).astype(BF16)
        out = jnp.dot(h, w3v[...], preferred_element_type=F32) * jnp.sqrt(ard[...])
        return out.astype(BF16)

    def half_sq(feats):
        f = feats.astype(F32)
        return (-0.5 * LOG2E) * jnp.sum(f * f, axis=1, keepdims=True)

    def embed_cols(*slots):
        points = jnp.concatenate([xc[s, 0:64, :] for s in slots], axis=1)
        pre = lax.dot_general(
            points, w1v[0:64, :], (((0,), (0,)), ((), ())), preferred_element_type=F32
        )
        feats = embed(pre)
        for i, s in enumerate(slots):
            part = feats[512 * i : 512 * i + 512]
            fc[512 * s : 512 * s + 512, :] = part
            cn[512 * s : 512 * s + 512, :] = jnp.broadcast_to(half_sq(part), (512, 128))
            vct[:, 512 * s : 512 * s + 512] = xc[s, 64:128, :]
        done = []
        for s in slots:
            lo, hi = (slice(512 * s, 512 * s + 512), slice(2048 + 512 * s, 2560 + 512 * s))
            done.append(send(fc.at[lo], fc.at[hi], p_s.at[s], p_r.at[s], dev(other=1)))
            done.append(
                send(vct.at[:, lo], vct.at[:, hi], p_s.at[4 + s], p_r.at[4 + s], dev(other=1))
            )
        return done

    def embed_rows(*slots):
        raw = jnp.concatenate([xr[256 * s : 256 * s + 256, :] for s in slots], axis=0)
        feats = embed(jnp.dot(raw, w1v[...], preferred_element_type=F32))
        values = raw.T
        norms = jnp.broadcast_to(half_sq(feats), (256 * len(slots), 128)).T
        for i, s in enumerate(slots):
            here, there = (slice(256 * i, 256 * i + 256), slice(256 * s, 256 * s + 256))
            rf[there, :] = feats[here]
            vrt[:, there] = values[64:128, here]
            rn[:, there] = norms[0:8, here]

    def z_step(step):
        now = []
        for table, d in ((MINUS, 1), (PLUS, -1)):
            if step in table:
                a, b = (table[step - 1] * 256, table[step] * 256)
                i = table[step]
                now.append(
                    send(xr.at[a : a + 256], xr.at[b : b + 256], z_s.at[i], z_r.at[i], dev(dz=d))
                )
        return now

    def arrive(copies):
        for c in copies:
            c.wait_recv()

    def panel(p, lo, hi, first_rows, first_cols):
        r = slice(512 * p, 512 * p + 512)
        inner = lax.dot_general(
            fc[lo:hi, :], rf[r, :], (((1,), (1,)), ((), ())), preferred_element_type=F32
        )
        norms = jnp.concatenate([cn[lo:hi, :]] * 4, axis=1)
        k = jnp.exp2(inner * LOG2E + norms + rn[0:1, r]).astype(BF16)
        rows = jnp.dot(vct[:, lo:hi], k, preferred_element_type=F32)
        orr[:, r] = rows if first_rows else orr[:, r] + rows
        n = hi - lo
        pt[:, 0:n] = k.T
        cols = jnp.dot(vrt[:, r], pt[:, 0:n], preferred_element_type=F32)
        oc[:, lo:hi] = cols if first_cols else oc[:, lo:hi] + cols

    row_out, col_out = ([], [])

    def send_rows(p):
        rt = orr[:, 512 * p : 512 * p + 512].T.astype(BF16)
        for j in range(8):
            n = 8 * p + j
            rsend[n] = jnp.concatenate(
                [rt[64 * j : 64 * j + 32], rt[64 * j + 32 : 64 * j + 64]], axis=1
            )
        for j in range(8):
            n = 8 * p + j
            dz, dy = (Z_OFF[n // 4], Y_OFF[n % 4])
            if (dz, dy) != (0, 0):
                row_out.append(
                    send(rsend.at[n], rrecv.at[n], rr_s.at[n], rr_r.at[n], dev(dy=dy, dz=dz))
                )

    def send_cols(*slots):
        for n in slots:
            at = slice(512 * n, 512 * n + 512)
            csend[:, at] = oc[:, at].astype(BF16)
        for n in slots:
            at = slice(512 * n, 512 * n + 512)
            if n:
                to = dev(dx=X_OFF[n % 4], other=n // 4)
                col_out.append(send(csend.at[:, at], crecv.at[n], cc_s.at[n], cc_r.at[n], to))

    partner = embed_cols(0)
    arrive(ys)
    z1 = z_step(1)
    embed_rows(7)
    xs[2, 0].wait_recv()
    xs[3, 0] = send(half(2, 0), half(3, 0), x_s.at[6], x_r.at[6], dev(dx=1))
    xs[1, 1].wait_recv()
    xs[3, 1] = send(half(1, 1), half(3, 1), x_s.at[7], x_r.at[7], dev(dx=-1))
    arrive([xs[2, 1], xs[1, 0]])
    partner += embed_cols(1, 2)
    arrive(z1)
    z2 = z_step(2)
    embed_rows(6, 5)
    arrive([xs[3, 0], xs[3, 1]])
    partner += embed_cols(3)
    arrive(z2)
    z3 = z_step(3)
    embed_rows(4, 1)
    panel(3, 0, 2048, True, True)
    arrive(z3)
    z4 = z_step(4)
    embed_rows(0, 3)
    panel(2, 0, 2048, True, False)
    panel(0, 0, 2048, True, False)
    arrive(z4)
    embed_rows(2)
    panel(1, 0, 2048, True, False)
    send_cols(3, 2, 1, 0)
    arrive(partner)
    for s in range(4, 8):
        at = slice(512 * s, 512 * s + 512)
        cn[at, :] = jnp.broadcast_to(half_sq(fc[at, :]), (512, 128))
    panel(1, 2048, 4096, False, True)
    send_rows(1)
    panel(0, 2048, 4096, False, False)
    send_rows(0)
    panel(2, 3072, 4096, False, False)
    panel(3, 3072, 4096, False, False)
    send_cols(7, 6)
    panel(2, 2048, 3072, False, False)
    send_rows(2)
    panel(3, 2048, 3072, False, False)
    send_cols(5, 4)
    send_rows(3)

    scale = sig[0]
    arrive(row_out)
    total = rsend[28].astype(F32)
    for n in range(32):
        if n != 28:
            total += rrecv[n].astype(F32)
    total = total * scale
    rout[0:32, :] = total[:, 0:64]
    rout[32:64, :] = total[:, 64:128]
    arrive(col_out)
    total = csend[:, 0:512].astype(F32)
    for n in range(1, 8):
        total += crecv[n].astype(F32)
    cout[...] = total * scale
    for c in sent:
        c.wait_send()


def body(rp, cp, rv, cv, w1, b1, w2, b2, w3, ard, sig):
    vmem = pl.BlockSpec(memory_space=pltpu.VMEM)
    away = pl.BlockSpec(memory_space=pl.ANY)
    dma = pltpu.SemaphoreType.DMA
    rows, cols = pl.pallas_call(
        kernel,
        out_shape=(jax.ShapeDtypeStruct((64, 64), F32), jax.ShapeDtypeStruct((64, 512), F32)),
        in_specs=[away] * 5 + [vmem, away, vmem, away, vmem, pl.BlockSpec(memory_space=pltpu.SMEM)],
        out_specs=(vmem, vmem),
        scratch_shapes=[
            pltpu.VMEM((128, 512), BF16),
            pltpu.VMEM((512, 512), BF16),
            pltpu.VMEM((512, 256), BF16),
            pltpu.VMEM((64, 64), BF16),
            pltpu.VMEM((64, 64), BF16),
            pltpu.VMEM((2048, 128), BF16),
            pltpu.VMEM((4, 128, 512), BF16),
            pltpu.VMEM((2048, 256), BF16),
            pltpu.VMEM((4096, 256), BF16),
            pltpu.VMEM((64, 2048), BF16),
            pltpu.VMEM((64, 4096), BF16),
            pltpu.VMEM((8, 2048), F32),
            pltpu.VMEM((4096, 128), F32),
            pltpu.VMEM((512, 2048), BF16),
            pltpu.VMEM((64, 4096), F32),
            pltpu.VMEM((64, 2048), F32),
            pltpu.VMEM((32, 32, 128), BF16),
            pltpu.VMEM((32, 32, 128), BF16),
            pltpu.VMEM((64, 4096), BF16),
            pltpu.VMEM((8, 64, 512), BF16),
            dma((7,)), dma((4,)), dma((4,)), dma((8,)), dma((8,)), dma((8,)), dma((8,)),
            dma((8,)), dma((8,)), dma((32,)), dma((32,)), dma((8,)), dma((8,)),
        ],
        compiler_params=pltpu.CompilerParams(
            collective_id=0, has_side_effects=True, vmem_limit_bytes=62 * 2**20
        ),
    )(
        rp, rv, cp.T, cv.T, w1, b1.reshape(1, -1), w2, b2.reshape(1, -1), w3,
        ard.reshape(1, -1), sig,
    )
    return (rows, cols.T)


def solution(mesh):
    rows, cols = (P(("row", "col"), None), P(("col", "row"), None))
    in_specs = (rows, cols, rows, cols) + (P(),) * 7
    return jax.shard_map(
        body, mesh=mesh, in_specs=in_specs, out_specs=(rows, cols), check_vma=False
    )
```

```python
import jax
import jax.numpy as jnp
from jax import lax
from jax.experimental import pallas as pl
from jax.experimental.pallas import tpu as pltpu
from jax.sharding import PartitionSpec as P

MESH = pl.DeviceIdType.MESH
F32 = jnp.float32
BF16 = jnp.bfloat16
LOG2E = 1.4426950408889634

NX, NY, NZ = (4, 4, 8)
Z_OFF = (0, -1, 1, -2, 2, -3, 3, 4)
Y_OFF = (0, -1, 1, 2)
X_OFF = (0, 1, -1, 2)
BATCHES = ((0, 3), (3, 5), (5, 8))


def kernel(
    rp, rv, cp, cv, w1, b1, w2, b2, w3, ard,
    rout, cout,
    w1v, w2v, w3v, rpv, rvv, xr, xc, rf, fc, vrt, vct, rn, cn, pt, oc, orr,
    rsend, rrecv, csend, crecv,
    l_s, y_s, y_r, z_s, z_r, x_s, x_r, p_s, p_r, rr_s, rr_r, cc_s, cc_r,
):
    row, col = (lax.axis_index("row"), lax.axis_index("col"))
    core = lax.rem(row, 2)
    y = lax.rem(lax.div(row, 2), NY)
    x = lax.div(row, 2 * NY) + 2 * lax.rem(col, 2)
    z = lax.div(col, 2)

    def dev(dx=0, dy=0, dz=0, other=0):
        px = lax.rem(x + (dx + NX), NX)
        py = lax.rem(y + (dy + NY), NY)
        pz = lax.rem(z + (dz + NZ), NZ)
        pc = 1 - core if other else core
        return (lax.rem(px, 2) * (2 * NY) + py * 2 + pc, pz * 2 + lax.div(px, 2))

    sent = []

    def send(src, dst, s, r, to):
        c = pltpu.make_async_remote_copy(
            src_ref=src, dst_ref=dst, send_sem=s, recv_sem=r, device_id=to, device_id_type=MESH
        )
        c.start()
        sent.append(c)
        return c

    peers = [dict(other=1)] + [dict(dx=d) for d in X_OFF[1:]]
    peers += [dict(dy=d) for d in Y_OFF[1:]] + [dict(dz=d) for d in Z_OFF[1:]]
    barrier = pltpu.get_barrier_semaphore()
    for q in peers:
        pl.semaphore_signal(barrier, inc=1, device_id=dev(**q), device_id_type=MESH)

    local = []
    for i, (a, b) in enumerate(
        ((rp, rpv), (rv, rvv), (cp, xc.at[0, 0:64]), (cv, xc.at[0, 64:128]), (w1, w1v.at[0:64]),
         (w2, w2v), (w3, w3v))
    ):
        c = pltpu.make_async_copy(a, b, l_s.at[i])
        c.start()
        local.append(c)
    w1v[64:128, :] = jnp.zeros((64, 512), BF16)
    local[0].wait()
    local[1].wait()
    xr[0:64, :] = jnp.concatenate([rpv[...], rvv[...]], axis=1)
    for c in local[2:]:
        c.wait()

    def embed(pre):
        h = jnp.tanh(pre + b1[...]).astype(BF16)
        h = jnp.tanh(jnp.dot(h, w2v[...], preferred_element_type=F32) + b2[...]).astype(BF16)
        out = jnp.dot(h, w3v[...], preferred_element_type=F32) * jnp.sqrt(ard[...])
        return out.astype(BF16)

    def half_sq(feats):
        f = feats.astype(F32)
        return (-0.5 * LOG2E) * jnp.sum(f * f, axis=1, keepdims=True)

    def embed_cols(*slots):
        points = jnp.concatenate([xc[s, 0:64, :] for s in slots], axis=1)
        pre = lax.dot_general(
            points, w1v[0:64, :], (((0,), (0,)), ((), ())), preferred_element_type=F32
        )
        feats = embed(pre)
        for i, s in enumerate(slots):
            part = feats[512 * i : 512 * i + 512]
            fc[512 * s : 512 * s + 512, :] = part
            cn[512 * s : 512 * s + 512, :] = jnp.broadcast_to(half_sq(part), (512, 128))
            vct[:, 512 * s : 512 * s + 512] = xc[s, 64:128, :]

    def share_cols(*slots):
        done = []
        for s in slots:
            lo, hi = (slice(512 * s, 512 * s + 512), slice(2048 + 512 * s, 2560 + 512 * s))
            done.append(send(fc.at[lo], fc.at[hi], p_s.at[s], p_r.at[s], dev(other=1)))
            done.append(
                send(vct.at[:, lo], vct.at[:, hi], p_s.at[4 + s], p_r.at[4 + s], dev(other=1))
            )
        return done

    def embed_rows(p):
        at = slice(512 * p, 512 * p + 512)
        raw = xr[at, :]
        feats = embed(jnp.dot(raw, w1v[...], preferred_element_type=F32))
        rf[at, :] = feats
        vrt[:, at] = raw.T[64:128, :]
        rn[:, at] = jnp.broadcast_to(half_sq(feats), (512, 128)).T[0:8, :]

    def arrive(copies):
        for c in copies:
            c.wait_recv()

    def panel(p, lo, hi, first_rows, first_cols):
        r = slice(512 * p, 512 * p + 512)
        inner = lax.dot_general(
            fc[lo:hi, :], rf[r, :], (((1,), (1,)), ((), ())), preferred_element_type=F32
        )
        norms = jnp.concatenate([cn[lo:hi, :]] * 4, axis=1)
        k = jnp.exp2(inner * LOG2E + norms + rn[0:1, r]).astype(BF16)
        rows = jnp.dot(vct[:, lo:hi], k, preferred_element_type=F32)
        orr[:, r] = rows if first_rows else orr[:, r] + rows
        n = hi - lo
        pt[:, 0:n] = k.T
        cols = jnp.dot(vrt[:, r], pt[:, 0:n], preferred_element_type=F32)
        if first_cols is True:
            oc[:, lo:hi] = cols
        elif first_cols:
            m = first_cols[1]
            oc[:, lo:m] += cols[:, 0 : m - lo]
            oc[:, m:hi] = cols[:, m - lo :]
        else:
            oc[:, lo:hi] += cols

    row_out, col_out = ([], [])

    def send_rows(p):
        rt = orr[:, 512 * p : 512 * p + 512].T.astype(BF16)
        for j in range(8):
            n = 8 * p + j
            rsend[n] = jnp.concatenate(
                [rt[64 * j : 64 * j + 32], rt[64 * j + 32 : 64 * j + 64]], axis=1
            )
        for j in range(8):
            n = 8 * p + j
            dz, dy = (Z_OFF[n % 8], Y_OFF[n // 8])
            if (dz, dy) != (0, 0):
                row_out.append(
                    send(rsend.at[n], rrecv.at[n], rr_s.at[n], rr_r.at[n], dev(dy=dy, dz=dz))
                )

    def send_cols(*slots):
        for n in slots:
            at = slice(512 * n, 512 * n + 512)
            csend[:, at] = oc[:, at].astype(BF16)
        for n in slots:
            at = slice(512 * n, 512 * n + 512)
            if n:
                to = dev(dx=X_OFF[n % 4], other=n // 4)
                col_out.append(send(csend.at[:, at], crecv.at[n], cc_s.at[n], cc_r.at[n], to))

    embed_cols(0)
    pl.semaphore_wait(barrier, len(peers))
    zs = []
    for i, d in enumerate(Z_OFF):
        if i:
            zs.append(
                send(xr.at[0:64], xr.at[64 * i : 64 * i + 64], z_s.at[i], z_r.at[i], dev(dz=-d))
            )
    xs = [None]
    for j, d in enumerate(X_OFF):
        if j:
            xs.append(send(xc.at[0], xc.at[j], x_s.at[j], x_r.at[j], dev(dx=-d)))
    partner = share_cols(0)
    ys = {1: [], 2: [], 3: []}
    for n, (lo, hi) in enumerate(BATCHES):
        arrive(zs[max(lo, 1) - 1 : hi - 1])
        for j, d in enumerate(Y_OFF):
            if j:
                i = 3 * j + n
                a, b = (slice(64 * lo, 64 * hi), slice(512 * j + 64 * lo, 512 * j + 64 * hi))
                ys[j].append(send(xr.at[a], xr.at[b], y_s.at[i], y_r.at[i], dev(dy=-d)))
    embed_rows(0)
    arrive(xs[1:3])
    embed_cols(1, 2)
    partner += share_cols(1, 2)
    panel(0, 0, 1536, True, True)
    arrive(xs[3:])
    embed_cols(3)
    partner += share_cols(3)
    arrive(ys[1])
    embed_rows(1)
    panel(1, 0, 2048, True, (0, 1536))
    arrive(ys[2])
    embed_rows(2)
    panel(2, 0, 2048, True, False)
    arrive(ys[3])
    embed_rows(3)
    panel(3, 0, 2048, True, False)
    panel(0, 1536, 2048, False, False)
    send_cols(3, 2, 1, 0)
    arrive(partner)
    for s in range(4, 8):
        at = slice(512 * s, 512 * s + 512)
        cn[at, :] = jnp.broadcast_to(half_sq(fc[at, :]), (512, 128))
    panel(3, 2048, 4096, False, True)
    send_rows(3)
    panel(2, 2048, 4096, False, False)
    send_rows(2)
    panel(1, 3072, 4096, False, False)
    panel(0, 3072, 4096, False, False)
    send_cols(7, 6)
    panel(1, 2048, 3072, False, False)
    send_rows(1)
    panel(0, 2048, 3072, False, False)
    send_cols(5, 4)
    send_rows(0)

    arrive(row_out)
    total = rsend[0].astype(F32)
    for n in range(1, 32):
        total += rrecv[n].astype(F32)
    rout[0:32, :] = total[:, 0:64]
    rout[32:64, :] = total[:, 64:128]
    arrive(col_out)
    total = csend[:, 0:512].astype(F32)
    for n in range(1, 8):
        total += crecv[n].astype(F32)
    cout[...] = total
    for c in sent:
        c.wait_send()


def finish(rin, cin, sig, rout, cout):
    rout[...] = rin[...] * sig[0]
    cout[...] = cin[...] * sig[0]


def body(rp, cp, rv, cv, w1, b1, w2, b2, w3, ard, sig):
    vmem = pl.BlockSpec(memory_space=pltpu.VMEM)
    away = pl.BlockSpec(memory_space=pl.ANY)
    dma = pltpu.SemaphoreType.DMA
    rows, cols = pl.pallas_call(
        kernel,
        out_shape=(jax.ShapeDtypeStruct((64, 64), F32), jax.ShapeDtypeStruct((64, 512), F32)),
        in_specs=[away] * 5 + [vmem, away, vmem, away, vmem],
        out_specs=(vmem, vmem),
        scratch_shapes=[
            pltpu.VMEM((128, 512), BF16),
            pltpu.VMEM((512, 512), BF16),
            pltpu.VMEM((512, 256), BF16),
            pltpu.VMEM((64, 64), BF16),
            pltpu.VMEM((64, 64), BF16),
            pltpu.VMEM((2048, 128), BF16),
            pltpu.VMEM((4, 128, 512), BF16),
            pltpu.VMEM((2048, 256), BF16),
            pltpu.VMEM((4096, 256), BF16),
            pltpu.VMEM((64, 2048), BF16),
            pltpu.VMEM((64, 4096), BF16),
            pltpu.VMEM((8, 2048), F32),
            pltpu.VMEM((4096, 128), F32),
            pltpu.VMEM((512, 2048), BF16),
            pltpu.VMEM((64, 4096), F32),
            pltpu.VMEM((64, 2048), F32),
            pltpu.VMEM((32, 32, 128), BF16),
            pltpu.VMEM((32, 32, 128), BF16),
            pltpu.VMEM((64, 4096), BF16),
            pltpu.VMEM((8, 64, 512), BF16),
            dma((7,)), dma((12,)), dma((12,)), dma((8,)), dma((8,)), dma((4,)), dma((4,)),
            dma((8,)), dma((8,)), dma((32,)), dma((32,)), dma((8,)), dma((8,)),
        ],
        compiler_params=pltpu.CompilerParams(
            collective_id=0, has_side_effects=True, vmem_limit_bytes=62 * 2**20
        ),
    )(
        rp, rv, cp.T, cv.T, w1, b1.reshape(1, -1), w2, b2.reshape(1, -1), w3,
        ard.reshape(1, -1),
    )
    rows, cols = pl.pallas_call(
        finish,
        out_shape=(jax.ShapeDtypeStruct((64, 64), F32), jax.ShapeDtypeStruct((64, 512), F32)),
        in_specs=[vmem, vmem, pl.BlockSpec(memory_space=pltpu.SMEM)],
        out_specs=(vmem, vmem),
    )(rows, cols, sig)
    return (rows, cols.T)


def solution(mesh):
    rows, cols = (P(("row", "col"), None), P(("col", "row"), None))
    in_specs = (rows, cols, rows, cols) + (P(),) * 7
    return jax.shard_map(
        body, mesh=mesh, in_specs=in_specs, out_specs=(rows, cols), check_vma=False
    )
```

```python
import jax
import jax.numpy as jnp
from jax import lax
from jax.experimental import pallas as pl
from jax.experimental.pallas import tpu as pltpu
from jax.sharding import PartitionSpec as P

MESH = pl.DeviceIdType.MESH
F32 = jnp.float32
BF16 = jnp.bfloat16
LOG2E = 1.4426950408889634

NX, NY, NZ = (4, 4, 8)
Z_OFF = (0, -1, 1, -2, 2, -3, 3, 4)
Y_OFF = (0, -1, 1, 2)
X_OFF = (0, 1, -1, 2)
BLOCKS = tuple((i, 0) for i in range(8)) + tuple((i, j) for i in range(8) for j in (1, 2, 3))
BATCHES = ((0, 3), (3, 5), (5, 8))


def kernel(
    rp, rv, cp, cv, w1, b1h, w2, b2h, w3, ardh,
    rout, cout,
    w1v, w2v, w3v, b1, b2, ard, rpv, rvv, xr, xo, xc, rf, fc, vrt, vct, rn, cn, pt, oc, orr,
    rsend, rrecv, csend, crecv,
    l_s, y_s, y_r, z_s, z_r, x_s, x_r, p_s, p_r, rr_s, rr_r, cc_s, cc_r,
):
    row, col = (lax.axis_index("row"), lax.axis_index("col"))
    core = lax.rem(row, 2)
    y = lax.rem(lax.div(row, 2), NY)
    x = lax.div(row, 2 * NY) + 2 * lax.rem(col, 2)
    z = lax.div(col, 2)

    def dev(dx=0, dy=0, dz=0, other=0):
        px = lax.rem(x + (dx + NX), NX)
        py = lax.rem(y + (dy + NY), NY)
        pz = lax.rem(z + (dz + NZ), NZ)
        pc = 1 - core if other else core
        return (lax.rem(px, 2) * (2 * NY) + py * 2 + pc, pz * 2 + lax.div(px, 2))

    sent = []

    def send(src, dst, s, r, to):
        c = pltpu.make_async_remote_copy(
            src_ref=src, dst_ref=dst, send_sem=s, recv_sem=r, device_id=to, device_id_type=MESH
        )
        c.start()
        sent.append(c)
        return c

    peers = [dict(other=1)] + [dict(dx=d) for d in X_OFF[1:]]
    peers += [dict(dy=d) for d in Y_OFF[1:]] + [dict(dz=d) for d in Z_OFF[1:]]
    barrier = pltpu.get_barrier_semaphore()
    for q in peers:
        pl.semaphore_signal(barrier, inc=1, device_id=dev(**q), device_id_type=MESH)

    local = []
    for i, (a, b) in enumerate(
        ((rp, rpv), (rv, rvv), (cp, xc.at[0, 0:64]), (cv, xc.at[0, 64:128]), (w1, w1v.at[0:64]),
         (w2, w2v), (w3, w3v), (b1h, b1), (b2h, b2), (ardh, ard))
    ):
        c = pltpu.make_async_copy(a, b, l_s.at[i])
        c.start()
        local.append(c)
    w1v[64:128, :] = jnp.zeros((64, 512), BF16)
    local[0].wait()
    local[1].wait()
    xr[0] = jnp.concatenate([rpv[...], rvv[...]], axis=1)
    for c in local[2:4]:
        c.wait()

    def embed(pre):
        h = jnp.tanh(pre + b1[...]).astype(BF16)
        h = jnp.tanh(jnp.dot(h, w2v[...], preferred_element_type=F32) + b2[...]).astype(BF16)
        out = jnp.dot(h, w3v[...], preferred_element_type=F32) * jnp.sqrt(ard[...])
        return out.astype(BF16)

    def half_sq(feats):
        f = feats.astype(F32)
        return (-0.5 * LOG2E) * jnp.sum(f * f, axis=1, keepdims=True)

    def embed_cols(n, *starts):
        blocks = [(at // 512, slice(at % 512, at % 512 + n)) for at in starts]
        points = jnp.concatenate([xc[j, 0:64, lanes] for j, lanes in blocks], axis=1)
        pre = lax.dot_general(
            points, w1v[0:64, :], (((0,), (0,)), ((), ())), preferred_element_type=F32
        )
        feats = embed(pre)
        for i, (at, (j, lanes)) in enumerate(zip(starts, blocks)):
            part = feats[n * i : n * i + n]
            fc[at : at + n, :] = part
            cn[at : at + n, :] = jnp.broadcast_to(half_sq(part), (n, 128))
            vct[:, at : at + n] = xc[j, 64:128, lanes]

    def share_cols(*slots):
        done = []
        for s in slots:
            lo, hi = (slice(512 * s, 512 * s + 512), slice(2048 + 512 * s, 2560 + 512 * s))
            done.append(send(fc.at[lo], fc.at[hi], p_s.at[s], p_r.at[s], dev(other=1)))
            done.append(
                send(vct.at[:, lo], vct.at[:, hi], p_s.at[4 + s], p_r.at[4 + s], dev(other=1))
            )
            done.append(send(cn.at[lo], cn.at[hi], p_s.at[8 + s], p_r.at[8 + s], dev(other=1)))
        return done

    def embed_rows(p):
        at = slice(512 * p, 512 * p + 512)
        blocks = BLOCKS[8 * p : 8 * p + 8]
        raw = jnp.concatenate([xo[i, j - 1] if j else xr[i] for i, j in blocks], axis=0)
        feats = embed(jnp.dot(raw, w1v[...], preferred_element_type=F32))
        rf[at, :] = feats
        vrt[:, at] = raw.T[64:128, :]
        rn[:, at] = jnp.broadcast_to(half_sq(feats), (512, 128)).T[0:8, :]

    def arrive(copies):
        for c in copies:
            c.wait_recv()

    turn = [0]

    def panel(p, lo, hi):
        first_rows, first_cols = (lo == 0, p == 0)
        turn[0] = 1 - turn[0]
        r = slice(512 * p, 512 * p + 512)
        inner = lax.dot_general(
            fc[lo:hi, :], rf[r, :], (((1,), (1,)), ((), ())), preferred_element_type=F32
        )
        norms = jnp.concatenate([cn[lo:hi, :]] * 4, axis=1)
        k = jnp.exp2(inner * LOG2E + norms + rn[0:1, r]).astype(BF16)
        rows = jnp.dot(vct[:, lo:hi], k, preferred_element_type=F32)
        orr[:, r] = rows if first_rows else orr[:, r] + rows
        n = hi - lo
        flip = pt.at[turn[0], :, 0:n]
        flip[...] = k.T
        cols = jnp.dot(vrt[:, r], flip[...], preferred_element_type=F32)
        oc[:, lo:hi] = cols if first_cols else oc[:, lo:hi] + cols

    row_out, col_out = ([], [])

    def send_rows(p):
        rt = orr[:, 512 * p : 512 * p + 512].T.astype(BF16)
        for j in range(8):
            n = 8 * p + j
            rsend[n] = jnp.concatenate(
                [rt[64 * j : 64 * j + 32], rt[64 * j + 32 : 64 * j + 64]], axis=1
            )
        for j in range(8):
            n = 8 * p + j
            dz, dy = (Z_OFF[BLOCKS[n][0]], Y_OFF[BLOCKS[n][1]])
            if (dz, dy) != (0, 0):
                row_out.append(
                    send(rsend.at[n], rrecv.at[n], rr_s.at[n], rr_r.at[n], dev(dy=dy, dz=dz))
                )

    def send_cols(*slots):
        for n in slots:
            at = slice(512 * n, 512 * n + 512)
            csend[:, at] = oc[:, at].astype(BF16)
        for n in slots:
            at = slice(512 * n, 512 * n + 512)
            if n:
                to = dev(dx=X_OFF[n % 4], other=n // 4)
                col_out.append(send(csend.at[:, at], crecv.at[n], cc_s.at[n], cc_r.at[n], to))

    pl.semaphore_wait(barrier, len(peers))
    zs = []
    for i, d in enumerate(Z_OFF):
        if i:
            zs.append(
                send(xr.at[0], xr.at[i], z_s.at[i], z_r.at[i], dev(dz=-d))
            )
    xs = {}
    for h in (0, 1):
        for j in (1, 2):
            part = (slice(None), slice(256 * h, 256 * h + 256))
            i = 2 * j + h
            xs[j, h] = send(
                xc.at[0].at[part], xc.at[j].at[part], x_s.at[i], x_r.at[i], dev(dx=-X_OFF[j])
            )
    xs[3] = send(xc.at[0], xc.at[3], x_s.at[0], x_r.at[0], dev(dx=-X_OFF[3]))
    for c in local[4:]:
        c.wait()
    embed_cols(512, 0)
    partner = share_cols(0)
    ys = []

    def relay(n):
        lo, hi = BATCHES[n]
        arrive(zs[max(lo, 1) - 1 : hi - 1])
        for j, d in enumerate(Y_OFF):
            if j:
                i = 3 * j + n
                a, b = (xr.at[lo:hi], xo.at[lo:hi, j - 1])
                ys.append(send(a, b, y_s.at[i], y_r.at[i], dev(dy=-d)))

    relay(0)
    arrive([xs[1, 0], xs[2, 0]])
    embed_cols(256, 512, 1024)
    relay(1)
    arrive([xs[1, 1], xs[2, 1]])
    embed_cols(256, 768, 1280)
    partner += share_cols(1, 2)
    relay(2)
    embed_rows(0)
    panel(0, 0, 1536)
    arrive([xs[3]])
    embed_cols(512, 1536)
    last = share_cols(3)
    arrive(partner)
    panel(0, 1536, 2048)
    panel(0, 2048, 3584)
    arrive(last)
    arrive(ys)
    panel(0, 3584, 4096)
    embed_rows(3)
    embed_rows(2)
    embed_rows(1)
    send_rows(0)
    panel(3, 0, 2048)
    panel(3, 2048, 4096)
    send_rows(3)
    panel(2, 0, 2048)
    panel(1, 0, 2048)
    send_cols(3, 2, 1, 0)
    panel(2, 2048, 4096)
    panel(1, 3072, 4096)
    send_rows(2)
    send_cols(7, 6)
    panel(1, 2560, 3072)
    send_cols(5)
    panel(1, 2048, 2560)
    send_rows(1)
    send_cols(4)

    arrive(row_out)
    total = rsend[0].astype(F32)
    for n in range(1, 32):
        total += rrecv[n].astype(F32)
    rout[0:32, :] = total[:, 0:64]
    rout[32:64, :] = total[:, 64:128]
    arrive(col_out)
    total = csend[:, 0:512].astype(F32)
    for n in range(1, 8):
        total += crecv[n].astype(F32)
    cout[...] = total
    for c in sent:
        c.wait_send()


def finish(rin, cin, sig, rout, cout):
    rout[...] = rin[...] * sig[0]
    cout[...] = cin[...] * sig[0]


def body(rp, cp, rv, cv, w1, b1, w2, b2, w3, ard, sig):
    vmem = pl.BlockSpec(memory_space=pltpu.VMEM)
    away = pl.BlockSpec(memory_space=pl.ANY)
    dma = pltpu.SemaphoreType.DMA
    rows, cols = pl.pallas_call(
        kernel,
        out_shape=(jax.ShapeDtypeStruct((64, 64), F32), jax.ShapeDtypeStruct((64, 512), F32)),
        in_specs=[away] * 10,
        out_specs=(vmem, vmem),
        scratch_shapes=[
            pltpu.VMEM((128, 512), BF16),
            pltpu.VMEM((512, 512), BF16),
            pltpu.VMEM((512, 256), BF16),
            pltpu.VMEM((1, 512), F32),
            pltpu.VMEM((1, 512), F32),
            pltpu.VMEM((1, 256), F32),
            pltpu.VMEM((64, 64), BF16),
            pltpu.VMEM((64, 64), BF16),
            pltpu.VMEM((8, 64, 128), BF16),
            pltpu.VMEM((8, 3, 64, 128), BF16),
            pltpu.VMEM((4, 128, 512), BF16),
            pltpu.VMEM((2048, 256), BF16),
            pltpu.VMEM((4096, 256), BF16),
            pltpu.VMEM((64, 2048), BF16),
            pltpu.VMEM((64, 4096), BF16),
            pltpu.VMEM((8, 2048), F32),
            pltpu.VMEM((4096, 128), F32),
            pltpu.VMEM((2, 512, 2048), BF16),
            pltpu.VMEM((64, 4096), F32),
            pltpu.VMEM((64, 2048), F32),
            pltpu.VMEM((32, 32, 128), BF16),
            pltpu.VMEM((32, 32, 128), BF16),
            pltpu.VMEM((64, 4096), BF16),
            pltpu.VMEM((8, 64, 512), BF16),
            dma((10,)), dma((12,)), dma((12,)), dma((8,)), dma((8,)), dma((8,)), dma((8,)),
            dma((12,)), dma((12,)), dma((32,)), dma((32,)), dma((8,)), dma((8,)),
        ],
        compiler_params=pltpu.CompilerParams(
            collective_id=0, has_side_effects=True, vmem_limit_bytes=62 * 2**20
        ),
    )(
        rp, rv, cp.T, cv.T, w1, b1.reshape(1, -1), w2, b2.reshape(1, -1), w3,
        ard.reshape(1, -1),
    )
    rows, cols = pl.pallas_call(
        finish,
        out_shape=(jax.ShapeDtypeStruct((64, 64), F32), jax.ShapeDtypeStruct((64, 512), F32)),
        in_specs=[vmem, vmem, pl.BlockSpec(memory_space=pltpu.SMEM)],
        out_specs=(vmem, vmem),
    )(rows, cols, sig)
    return (rows, cols.T)


def solution(mesh):
    rows, cols = (P(("row", "col"), None), P(("col", "row"), None))
    in_specs = (rows, cols, rows, cols) + (P(),) * 7
    return jax.shard_map(
        body, mesh=mesh, in_specs=in_specs, out_specs=(rows, cols), check_vma=False
    )
```

```python
import jax
import jax.numpy as jnp
from jax import lax
from jax.experimental import pallas as pl
from jax.experimental.pallas import tpu as pltpu
from jax.sharding import PartitionSpec as P

MESH = pl.DeviceIdType.MESH
F32 = jnp.float32
BF16 = jnp.bfloat16
LOG2E = 1.4426950408889634

NX, NY, NZ = (4, 4, 8)
Z_OFF = (0, -1, 1, -2, 2, -3, 3, 4)
Y_OFF = (0, -1, 1, 2)
X_OFF = (0, 1, -1, 2)
BLOCKS = tuple((i, 0) for i in range(8)) + tuple((i, j) for i in range(8) for j in (1, 2, 3))
BATCHES = ((0, 3), (3, 5), (5, 8))


def kernel(
    rp, rv, cp, cv, w1, b1h, w2, b2h, w3, ardh, sig,
    rout, cout,
    w1v, w2v, w3v, b1, b2, ard, rpv, rvv, xr, xo, xc, rf, fc, vrt, vct, rn, cn, pt, oc, orr,
    rsend, rrecv, csend, crecv,
    l_s, y_s, y_r, z_s, z_r, x_s, x_r, p_s, p_r, rr_s, rr_r, cc_s, cc_r,
):
    row, col = (lax.axis_index("row"), lax.axis_index("col"))
    core = lax.rem(row, 2)
    y = lax.rem(lax.div(row, 2), NY)
    x = lax.div(row, 2 * NY) + 2 * lax.rem(col, 2)
    z = lax.div(col, 2)

    def dev(dx=0, dy=0, dz=0, other=0):
        px = lax.rem(x + (dx + NX), NX)
        py = lax.rem(y + (dy + NY), NY)
        pz = lax.rem(z + (dz + NZ), NZ)
        pc = 1 - core if other else core
        return (lax.rem(px, 2) * (2 * NY) + py * 2 + pc, pz * 2 + lax.div(px, 2))

    sent = []

    def send(src, dst, s, r, to):
        c = pltpu.make_async_remote_copy(
            src_ref=src, dst_ref=dst, send_sem=s, recv_sem=r, device_id=to, device_id_type=MESH
        )
        c.start()
        sent.append(c)
        return c

    peers = [dict(other=1)] + [dict(dx=d) for d in X_OFF[1:]]
    peers += [dict(dy=d) for d in Y_OFF[1:]] + [dict(dz=d) for d in Z_OFF[1:]]
    barrier = pltpu.get_barrier_semaphore()
    for q in peers:
        pl.semaphore_signal(barrier, inc=1, device_id=dev(**q), device_id_type=MESH)

    local = []
    for i, (a, b) in enumerate(
        ((rp, rpv), (rv, rvv), (cp, xc.at[0, 0:64]), (cv, xc.at[0, 64:128]), (w1, w1v.at[0:64]),
         (w2, w2v), (w3, w3v), (b1h, b1), (b2h, b2), (ardh, ard))
    ):
        c = pltpu.make_async_copy(a, b, l_s.at[i])
        c.start()
        local.append(c)
    w1v[64:128, :] = jnp.zeros((64, 512), BF16)
    local[0].wait()
    local[1].wait()
    xr[0] = jnp.concatenate([rpv[...], rvv[...]], axis=1)
    for c in local[2:4]:
        c.wait()

    def embed(pre):
        h = jnp.tanh(pre + b1[...]).astype(BF16)
        h = jnp.tanh(jnp.dot(h, w2v[...], preferred_element_type=F32) + b2[...]).astype(BF16)
        out = jnp.dot(h, w3v[...], preferred_element_type=F32) * jnp.sqrt(ard[...])
        return out.astype(BF16)

    def half_sq(feats):
        f = feats.astype(F32)
        return (-0.5 * LOG2E) * jnp.sum(f * f, axis=1, keepdims=True)

    def embed_cols(n, *starts):
        blocks = [(at // 512, slice(at % 512, at % 512 + n)) for at in starts]
        points = jnp.concatenate([xc[j, 0:64, lanes] for j, lanes in blocks], axis=1)
        pre = lax.dot_general(
            points, w1v[0:64, :], (((0,), (0,)), ((), ())), preferred_element_type=F32
        )
        feats = embed(pre)
        for i, (at, (j, lanes)) in enumerate(zip(starts, blocks)):
            part = feats[n * i : n * i + n]
            fc[at : at + n, :] = part
            cn[at : at + n, :] = jnp.broadcast_to(half_sq(part), (n, 128))
            vct[:, at : at + n] = xc[j, 64:128, lanes]

    def share_cols(*slots):
        done = []
        for s in slots:
            lo, hi = (slice(512 * s, 512 * s + 512), slice(2048 + 512 * s, 2560 + 512 * s))
            done.append(send(fc.at[lo], fc.at[hi], p_s.at[s], p_r.at[s], dev(other=1)))
            done.append(
                send(vct.at[:, lo], vct.at[:, hi], p_s.at[4 + s], p_r.at[4 + s], dev(other=1))
            )
            done.append(send(cn.at[lo], cn.at[hi], p_s.at[8 + s], p_r.at[8 + s], dev(other=1)))
        return done

    def embed_rows(p):
        at = slice(512 * p, 512 * p + 512)
        blocks = BLOCKS[8 * p : 8 * p + 8]
        raw = jnp.concatenate([xo[i, j - 1] if j else xr[i] for i, j in blocks], axis=0)
        feats = embed(jnp.dot(raw, w1v[...], preferred_element_type=F32))
        rf[at, :] = feats
        vrt[:, at] = raw.T[64:128, :]
        rn[:, at] = jnp.broadcast_to(half_sq(feats), (512, 128)).T[0:8, :]

    def arrive(copies):
        for c in copies:
            c.wait_recv()

    turn = [0]

    def panel(p, lo, hi):
        first_rows, first_cols = (lo == 0, p == 0)
        turn[0] = 1 - turn[0]
        r = slice(512 * p, 512 * p + 512)
        inner = lax.dot_general(
            fc[lo:hi, :], rf[r, :], (((1,), (1,)), ((), ())), preferred_element_type=F32
        )
        norms = jnp.concatenate([cn[lo:hi, :]] * 4, axis=1)
        k = jnp.exp2(inner * LOG2E + norms + rn[0:1, r]).astype(BF16)
        rows = jnp.dot(vct[:, lo:hi], k, preferred_element_type=F32)
        orr[:, r] = rows if first_rows else orr[:, r] + rows
        n = hi - lo
        flip = pt.at[turn[0], :, 0:n]
        flip[...] = k.T
        cols = jnp.dot(vrt[:, r], flip[...], preferred_element_type=F32)
        oc[:, lo:hi] = cols if first_cols else oc[:, lo:hi] + cols

    row_out, col_out = ([], [])

    def send_rows(p):
        rt = orr[:, 512 * p : 512 * p + 512].T.astype(BF16)
        for j in range(8):
            n = 8 * p + j
            rsend[n] = jnp.concatenate(
                [rt[64 * j : 64 * j + 32], rt[64 * j + 32 : 64 * j + 64]], axis=1
            )
        for j in range(8):
            n = 8 * p + j
            dz, dy = (Z_OFF[BLOCKS[n][0]], Y_OFF[BLOCKS[n][1]])
            if (dz, dy) != (0, 0):
                row_out.append(
                    send(rsend.at[n], rrecv.at[n], rr_s.at[n], rr_r.at[n], dev(dy=dy, dz=dz))
                )

    def send_cols(*slots):
        for n in slots:
            at = slice(512 * n, 512 * n + 512)
            csend[:, at] = oc[:, at].astype(BF16)
        for n in slots:
            at = slice(512 * n, 512 * n + 512)
            if n:
                to = dev(dx=X_OFF[n % 4], other=n // 4)
                col_out.append(send(csend.at[:, at], crecv.at[n], cc_s.at[n], cc_r.at[n], to))

    pl.semaphore_wait(barrier, len(peers))
    zs = []
    for i, d in enumerate(Z_OFF):
        if i:
            zs.append(
                send(xr.at[0], xr.at[i], z_s.at[i], z_r.at[i], dev(dz=-d))
            )
    xs = {}
    for h in (0, 1):
        for j in (1, 2):
            part = (slice(None), slice(256 * h, 256 * h + 256))
            i = 2 * j + h
            xs[j, h] = send(
                xc.at[0].at[part], xc.at[j].at[part], x_s.at[i], x_r.at[i], dev(dx=-X_OFF[j])
            )
    xs[3] = send(xc.at[0], xc.at[3], x_s.at[0], x_r.at[0], dev(dx=-X_OFF[3]))
    for c in local[4:]:
        c.wait()
    embed_cols(512, 0)
    partner = share_cols(0)
    ys = []

    def relay(n):
        lo, hi = BATCHES[n]
        arrive(zs[max(lo, 1) - 1 : hi - 1])
        for j, d in enumerate(Y_OFF):
            if j:
                i = 3 * j + n
                a, b = (xr.at[lo:hi], xo.at[lo:hi, j - 1])
                ys.append(send(a, b, y_s.at[i], y_r.at[i], dev(dy=-d)))

    relay(0)
    arrive([xs[1, 0], xs[2, 0]])
    embed_cols(256, 512, 1024)
    relay(1)
    arrive([xs[1, 1], xs[2, 1]])
    embed_cols(256, 768, 1280)
    partner += share_cols(1, 2)
    relay(2)
    embed_rows(0)
    panel(0, 0, 1536)
    arrive([xs[3]])
    embed_cols(512, 1536)
    last = share_cols(3)
    arrive(partner)
    panel(0, 1536, 2048)
    panel(0, 2048, 3584)
    arrive(last)
    arrive(ys)
    panel(0, 3584, 4096)
    embed_rows(3)
    embed_rows(2)
    embed_rows(1)
    send_rows(0)
    panel(3, 0, 2048)
    panel(3, 2048, 4096)
    send_rows(3)
    panel(2, 0, 2048)
    panel(1, 0, 2048)
    send_cols(3, 2, 1, 0)
    panel(2, 2048, 4096)
    panel(1, 3072, 4096)
    send_rows(2)
    send_cols(7, 6)
    panel(1, 2560, 3072)
    send_cols(5)
    panel(1, 2048, 2560)
    send_rows(1)
    send_cols(4)

    scale = sig[0]
    arrive(row_out)
    total = rsend[0].astype(F32)
    for n in range(1, 32):
        total += rrecv[n].astype(F32)
    total = total * scale
    rout[0:32, :] = total[:, 0:64]
    rout[32:64, :] = total[:, 64:128]
    arrive(col_out)
    total = csend[:, 0:512].astype(F32)
    for n in range(1, 8):
        total += crecv[n].astype(F32)
    cout[...] = total * scale
    for c in sent:
        c.wait_send()


def body(rp, cp, rv, cv, w1, b1, w2, b2, w3, ard, sig):
    vmem = pl.BlockSpec(memory_space=pltpu.VMEM)
    away = pl.BlockSpec(memory_space=pl.ANY)
    dma = pltpu.SemaphoreType.DMA
    rows, cols = pl.pallas_call(
        kernel,
        out_shape=(jax.ShapeDtypeStruct((64, 64), F32), jax.ShapeDtypeStruct((64, 512), F32)),
        in_specs=[away] * 10 + [pl.BlockSpec(memory_space=pltpu.SMEM)],
        out_specs=(vmem, vmem),
        scratch_shapes=[
            pltpu.VMEM((128, 512), BF16),
            pltpu.VMEM((512, 512), BF16),
            pltpu.VMEM((512, 256), BF16),
            pltpu.VMEM((1, 512), F32),
            pltpu.VMEM((1, 512), F32),
            pltpu.VMEM((1, 256), F32),
            pltpu.VMEM((64, 64), BF16),
            pltpu.VMEM((64, 64), BF16),
            pltpu.VMEM((8, 64, 128), BF16),
            pltpu.VMEM((8, 3, 64, 128), BF16),
            pltpu.VMEM((4, 128, 512), BF16),
            pltpu.VMEM((2048, 256), BF16),
            pltpu.VMEM((4096, 256), BF16),
            pltpu.VMEM((64, 2048), BF16),
            pltpu.VMEM((64, 4096), BF16),
            pltpu.VMEM((8, 2048), F32),
            pltpu.VMEM((4096, 128), F32),
            pltpu.VMEM((2, 512, 2048), BF16),
            pltpu.VMEM((64, 4096), F32),
            pltpu.VMEM((64, 2048), F32),
            pltpu.VMEM((32, 32, 128), BF16),
            pltpu.VMEM((32, 32, 128), BF16),
            pltpu.VMEM((64, 4096), BF16),
            pltpu.VMEM((8, 64, 512), BF16),
            dma((10,)), dma((12,)), dma((12,)), dma((8,)), dma((8,)), dma((8,)), dma((8,)),
            dma((12,)), dma((12,)), dma((32,)), dma((32,)), dma((8,)), dma((8,)),
        ],
        compiler_params=pltpu.CompilerParams(
            collective_id=0, has_side_effects=True, vmem_limit_bytes=40 * 2**20
        ),
    )(
        *(
            pltpu.with_memory_space_constraint(a, pltpu.HBM)
            for a in (
                rp, rv, cp.T, cv.T, w1, b1.reshape(1, -1), w2, b2.reshape(1, -1), w3,
                ard.reshape(1, -1),
            )
        ),
        sig,
    )
    return (rows, cols.T)


def solution(mesh):
    rows, cols = (P(("row", "col"), None), P(("col", "row"), None))
    in_specs = (rows, cols, rows, cols) + (P(),) * 7
    return jax.shard_map(
        body, mesh=mesh, in_specs=in_specs, out_specs=(rows, cols), check_vma=False
    )
```

```python
import jax
import jax.numpy as jnp
from jax import lax
from jax.experimental import pallas as pl
from jax.experimental.pallas import tpu as pltpu
from jax.sharding import PartitionSpec as P

MESH = pl.DeviceIdType.MESH
F32 = jnp.float32
BF16 = jnp.bfloat16
LOG2E = 1.4426950408889634

NX, NY, NZ = (4, 4, 8)
Z_OFF = (0, -1, 1, -2, 2, -3, 3, 4)
Y_OFF = (0, -1, 1, 2)
X_OFF = (0, 1, -1, 2)
BLOCKS = tuple((i, 0) for i in range(8)) + tuple((i, j) for i in range(8) for j in (1, 2, 3))
BATCHES = ((0, 3), (3, 5), (5, 8))


def kernel(
    rp, rv, cp, cv, w1, b1h, w2, b2h, w3, ardh, sig,
    rout, cout,
    w1v, w2v, w3v, b1, b2, ard, rpv, rvv, xr, xo, xc, rf, fc, vrt, vct, rn, cn, pt, oc, orr,
    rsend, rrecv, csend, crecv,
    l_s, y_s, y_r, z_s, z_r, x_s, x_r, p_s, p_r, rr_s, rr_r, cc_s, cc_r,
):
    row, col = (lax.axis_index("row"), lax.axis_index("col"))
    core = lax.rem(row, 2)
    y = lax.rem(lax.div(row, 2), NY)
    x = lax.div(row, 2 * NY) + 2 * lax.rem(col, 2)
    z = lax.div(col, 2)

    def dev(dx=0, dy=0, dz=0, other=0):
        px = lax.rem(x + (dx + NX), NX)
        py = lax.rem(y + (dy + NY), NY)
        pz = lax.rem(z + (dz + NZ), NZ)
        pc = 1 - core if other else core
        return (lax.rem(px, 2) * (2 * NY) + py * 2 + pc, pz * 2 + lax.div(px, 2))

    sent = []

    def send(src, dst, s, r, to):
        c = pltpu.make_async_remote_copy(
            src_ref=src, dst_ref=dst, send_sem=s, recv_sem=r, device_id=to, device_id_type=MESH
        )
        c.start()
        sent.append(c)
        return c

    peers = [dict(other=1)] + [dict(dx=d) for d in X_OFF[1:]]
    peers += [dict(dy=d) for d in Y_OFF[1:]] + [dict(dz=d) for d in Z_OFF[1:]]
    barrier = pltpu.get_barrier_semaphore()
    for q in peers:
        pl.semaphore_signal(barrier, inc=1, device_id=dev(**q), device_id_type=MESH)

    local = []
    for i, (a, b) in enumerate(
        ((rp, rpv), (rv, rvv), (cp, xc.at[0, 0:64]), (cv, xc.at[0, 64:128]), (w1, w1v.at[0:64]),
         (w2, w2v), (w3, w3v), (b1h, b1), (b2h, b2), (ardh, ard))
    ):
        c = pltpu.make_async_copy(a, b, l_s.at[i])
        c.start()
        local.append(c)
    w1v[64:128, :] = jnp.zeros((64, 512), BF16)
    local[0].wait()
    local[1].wait()
    xr[0] = jnp.concatenate([rpv[...], rvv[...]], axis=1)
    for c in local[2:4]:
        c.wait()

    def embed(pre):
        h = jnp.tanh(pre + b1[...]).astype(BF16)
        h = jnp.tanh(jnp.dot(h, w2v[...], preferred_element_type=F32) + b2[...]).astype(BF16)
        out = jnp.dot(h, w3v[...], preferred_element_type=F32) * jnp.sqrt(ard[...])
        return out.astype(BF16)

    def half_sq(feats):
        f = feats.astype(F32)
        return (-0.5 * LOG2E) * jnp.sum(f * f, axis=1, keepdims=True)

    def embed_cols(n, *starts):
        blocks = [(at // 512, slice(at % 512, at % 512 + n)) for at in starts]
        points = jnp.concatenate([xc[j, 0:64, lanes] for j, lanes in blocks], axis=1)
        pre = lax.dot_general(
            points, w1v[0:64, :], (((0,), (0,)), ((), ())), preferred_element_type=F32
        )
        feats = embed(pre)
        for i, (at, (j, lanes)) in enumerate(zip(starts, blocks)):
            part = feats[n * i : n * i + n]
            fc[at : at + n, :] = part
            cn[at : at + n, :] = jnp.broadcast_to(half_sq(part), (n, 128))
            vct[:, at : at + n] = xc[j, 64:128, lanes]

    def share_cols(*slots):
        done = []
        for s in slots:
            lo, hi = (slice(512 * s, 512 * s + 512), slice(2048 + 512 * s, 2560 + 512 * s))
            done.append(send(fc.at[lo], fc.at[hi], p_s.at[s], p_r.at[s], dev(other=1)))
            done.append(
                send(vct.at[:, lo], vct.at[:, hi], p_s.at[4 + s], p_r.at[4 + s], dev(other=1))
            )
            done.append(send(cn.at[lo], cn.at[hi], p_s.at[8 + s], p_r.at[8 + s], dev(other=1)))
        return done

    def embed_rows(p):
        at = slice(512 * p, 512 * p + 512)
        blocks = BLOCKS[8 * p : 8 * p + 8]
        raw = jnp.concatenate([xo[i, j - 1] if j else xr[i] for i, j in blocks], axis=0)
        feats = embed(jnp.dot(raw, w1v[...], preferred_element_type=F32))
        rf[at, :] = feats
        vrt[:, at] = raw.T[64:128, :]
        rn[:, at] = jnp.broadcast_to(half_sq(feats), (512, 128)).T[0:8, :]

    def arrive(copies):
        for c in copies:
            c.wait_recv()

    turn = [0]

    def panel(p, lo, hi):
        first_rows, first_cols = (lo == 0, p == 0)
        turn[0] = 1 - turn[0]
        r = slice(512 * p, 512 * p + 512)
        inner = lax.dot_general(
            fc[lo:hi, :], rf[r, :], (((1,), (1,)), ((), ())), preferred_element_type=F32
        )
        norms = jnp.concatenate([cn[lo:hi, :]] * 4, axis=1)
        k = jnp.exp2(inner * LOG2E + norms + rn[0:1, r]).astype(BF16)
        rows = jnp.dot(vct[:, lo:hi], k, preferred_element_type=F32)
        orr[:, r] = rows if first_rows else orr[:, r] + rows
        n = hi - lo
        flip = pt.at[turn[0], :, 0:n]
        flip[...] = k.T
        cols = jnp.dot(vrt[:, r], flip[...], preferred_element_type=F32)
        oc[:, lo:hi] = cols if first_cols else oc[:, lo:hi] + cols

    row_out, col_out = ([], [])

    def send_rows(p):
        rt = orr[:, 512 * p : 512 * p + 512].T.astype(BF16)
        for j in range(8):
            n = 8 * p + j
            rsend[n] = jnp.concatenate(
                [rt[64 * j : 64 * j + 32], rt[64 * j + 32 : 64 * j + 64]], axis=1
            )
        for j in range(8):
            n = 8 * p + j
            dz, dy = (Z_OFF[BLOCKS[n][0]], Y_OFF[BLOCKS[n][1]])
            if (dz, dy) != (0, 0):
                row_out.append(
                    send(rsend.at[n], rrecv.at[n], rr_s.at[n], rr_r.at[n], dev(dy=dy, dz=dz))
                )

    def send_cols(*slots):
        for n in slots:
            at = slice(512 * n, 512 * n + 512)
            csend[:, at] = oc[:, at].astype(BF16)
        for n in slots:
            at = slice(512 * n, 512 * n + 512)
            if n:
                to = dev(dx=X_OFF[n % 4], other=n // 4)
                col_out.append(send(csend.at[:, at], crecv.at[n], cc_s.at[n], cc_r.at[n], to))

    pl.semaphore_wait(barrier, len(peers))
    zs = []
    for i, d in enumerate(Z_OFF):
        if i:
            zs.append(
                send(xr.at[0], xr.at[i], z_s.at[i], z_r.at[i], dev(dz=-d))
            )
    xs = {}
    for h in (0, 1):
        for j in (1, 2):
            part = (slice(None), slice(256 * h, 256 * h + 256))
            i = 2 * j + h
            xs[j, h] = send(
                xc.at[0].at[part], xc.at[j].at[part], x_s.at[i], x_r.at[i], dev(dx=-X_OFF[j])
            )
    xs[3] = send(xc.at[0], xc.at[3], x_s.at[0], x_r.at[0], dev(dx=-X_OFF[3]))
    for c in local[4:]:
        c.wait()
    embed_cols(512, 0)
    partner = share_cols(0)
    ys = []

    def relay(n):
        lo, hi = BATCHES[n]
        arrive(zs[max(lo, 1) - 1 : hi - 1])
        for j, d in enumerate(Y_OFF):
            if j:
                i = 3 * j + n
                a, b = (xr.at[lo:hi], xo.at[lo:hi, j - 1])
                ys.append(send(a, b, y_s.at[i], y_r.at[i], dev(dy=-d)))

    relay(0)
    arrive([xs[1, 0], xs[2, 0]])
    embed_cols(256, 512, 1024)
    relay(1)
    arrive([xs[1, 1], xs[2, 1]])
    embed_cols(256, 768, 1280)
    partner += share_cols(1, 2)
    relay(2)
    embed_rows(0)
    panel(0, 0, 1536)
    arrive([xs[3]])
    embed_cols(512, 1536)
    last = share_cols(3)
    arrive(partner)
    panel(0, 1536, 3584)
    arrive(last)
    arrive(ys)
    panel(0, 3584, 4096)
    embed_rows(3)
    embed_rows(2)
    embed_rows(1)
    send_rows(0)
    panel(3, 0, 2048)
    panel(3, 2048, 4096)
    send_rows(3)
    panel(2, 0, 2048)
    panel(1, 0, 2048)
    send_cols(3, 2, 1, 0)
    panel(2, 2048, 4096)
    send_rows(2)
    panel(1, 3072, 4096)
    send_cols(7, 6)
    panel(1, 2048, 3072)
    send_rows(1)
    send_cols(5, 4)

    scale = sig[0]
    arrive(row_out)
    total = rsend[0].astype(F32)
    for n in range(1, 32):
        total += rrecv[n].astype(F32)
    total = total * scale
    rout[0:32, :] = total[:, 0:64]
    rout[32:64, :] = total[:, 64:128]
    arrive(col_out)
    total = csend[:, 0:512].astype(F32)
    for n in range(1, 8):
        total += crecv[n].astype(F32)
    cout[...] = total * scale
    for c in sent:
        c.wait_send()


def body(rp, cp, rv, cv, w1, b1, w2, b2, w3, ard, sig):
    vmem = pl.BlockSpec(memory_space=pltpu.VMEM)
    away = pl.BlockSpec(memory_space=pl.ANY)
    dma = pltpu.SemaphoreType.DMA
    rows, cols = pl.pallas_call(
        kernel,
        out_shape=(jax.ShapeDtypeStruct((64, 64), F32), jax.ShapeDtypeStruct((64, 512), F32)),
        in_specs=[away] * 10 + [pl.BlockSpec(memory_space=pltpu.SMEM)],
        out_specs=(vmem, vmem),
        scratch_shapes=[
            pltpu.VMEM((128, 512), BF16),
            pltpu.VMEM((512, 512), BF16),
            pltpu.VMEM((512, 256), BF16),
            pltpu.VMEM((1, 512), F32),
            pltpu.VMEM((1, 512), F32),
            pltpu.VMEM((1, 256), F32),
            pltpu.VMEM((64, 64), BF16),
            pltpu.VMEM((64, 64), BF16),
            pltpu.VMEM((8, 64, 128), BF16),
            pltpu.VMEM((8, 3, 64, 128), BF16),
            pltpu.VMEM((4, 128, 512), BF16),
            pltpu.VMEM((2048, 256), BF16),
            pltpu.VMEM((4096, 256), BF16),
            pltpu.VMEM((64, 2048), BF16),
            pltpu.VMEM((64, 4096), BF16),
            pltpu.VMEM((8, 2048), F32),
            pltpu.VMEM((4096, 128), F32),
            pltpu.VMEM((2, 512, 2048), BF16),
            pltpu.VMEM((64, 4096), F32),
            pltpu.VMEM((64, 2048), F32),
            pltpu.VMEM((32, 32, 128), BF16),
            pltpu.VMEM((32, 32, 128), BF16),
            pltpu.VMEM((64, 4096), BF16),
            pltpu.VMEM((8, 64, 512), BF16),
            dma((10,)), dma((12,)), dma((12,)), dma((8,)), dma((8,)), dma((8,)), dma((8,)),
            dma((12,)), dma((12,)), dma((32,)), dma((32,)), dma((8,)), dma((8,)),
        ],
        compiler_params=pltpu.CompilerParams(
            collective_id=0, has_side_effects=True, vmem_limit_bytes=40 * 2**20
        ),
    )(
        *(
            pltpu.with_memory_space_constraint(a, pltpu.HBM)
            for a in (
                rp, rv, cp.T, cv.T, w1, b1.reshape(1, -1), w2, b2.reshape(1, -1), w3,
                ard.reshape(1, -1),
            )
        ),
        sig,
    )
    return (rows, cols.T)


def solution(mesh):
    rows, cols = (P(("row", "col"), None), P(("col", "row"), None))
    in_specs = (rows, cols, rows, cols) + (P(),) * 7
    return jax.shard_map(
        body, mesh=mesh, in_specs=in_specs, out_specs=(rows, cols), check_vma=False
    )
```
